128 devices in a mesh: dp: 16 (over y, z), mp: 8 (over x, core).
Axes of the slice: x: 4, y: 4, z: 4, core: 2. Of those that a mesh axis runs over, the one named last changes fastest.
Arguments:
- grad_out: bfloat16 [16384, 6144], P(('dp', 'mp')), may hold values from -40 to 40
- context: bfloat16 [16384, 6144], P('dp', 'mp'), may hold values from -47 to 47
- weight: bfloat16 [6144, 6144], P(None, 'mp'), may hold values from -0.078125 to 0.078125
- master: float32 [6144, 6144], P('dp', 'mp'), may hold values from -0.6 to 0.6
- moment_q: bfloat16 [6144, 6144], P('dp', 'mp'), may hold values from -440 to 440
- second_moment: float32 [6144, 6144], P('dp', 'mp'), may hold values from 0.02 to 1
- moment_scale: float32 [], replicated, may hold values from 300 to 900
- scale_boost: float32 [], replicated, may hold values from 1.25 to 2
Outputs:
- input_grad: bfloat16 [16384, 6144], P('dp', 'mp')
- new_master: float32 [6144, 6144], P('dp', 'mp')
- new_moment_q: bfloat16 [6144, 6144], P('dp', 'mp')
- new_second: float32 [6144, 6144], P('dp', 'mp')
- new_scale: float32 [], replicated
- grad_scale: float32 [], replicated
- new_weight: bfloat16 [6144, 6144], P(None, 'mp')
The draws below stay inside these ranges and needn't reach their ends.
All inputs are finite; a program needn't handle non-finite values. Where the reference program divides by a largest or mean magnitude, that divisor is 1e-20 or more.
Results may differ from the reference program's by a relative error of at most 0.014.
Values may be sent and summed in bfloat16 or wider, within the bound.
No kernel may reach another device: no remote copies, remote signals or barrier semaphores. Data moves between devices by JAX's collectives and lax.ppermute only.
A program may use at most 128 MiB of HBM per device.

```python
import math
import jax
import jax.numpy as jnp
from jax import lax

D = 6144
TOK_DEV = 128
HD = 6144
TOKENS = 16384
N_DP = 16
N_MP = 8


def column_trend(key, count, span):
    position = jnp.arange(count, dtype=jnp.float32) / count
    rough = jnp.exp(jax.random.uniform(key, (count,), jnp.float32, 0.0, math.log(3.0)))
    return jnp.exp(position * math.log(span)) * rough


def trended_block(key, rows, count, factor):
    key_cols, key_base = jax.random.split(key, 2)
    columns = column_trend(key_cols, count, 3.0)
    base = jnp.clip(jax.random.normal(key_base, (rows, count), jnp.float32), -4.0, 4.0)
    return (base * columns * factor).astype(jnp.bfloat16)


def draw_grad_out(key, part):
    return trended_block(jax.random.fold_in(key, 11), TOKENS, D, 0.5)


def draw_context(key, part):
    return trended_block(jax.random.fold_in(key, 23), TOKENS, HD, 0.6)


def block_scale(own_key, extent, pieces, low, largest):
    level = 1.0
    for axis_at, shards_of in pieces:
        steps = jax.random.uniform(jax.random.fold_in(jax.random.fold_in(own_key, 6), axis_at), (shards_of,), jnp.float32, low / len(pieces), largest / len(pieces))
        level = level * jnp.repeat(jnp.exp(steps), extent[axis_at] // shards_of).reshape((-1,) + (1,) * (len(extent) - 1 - axis_at))
    return level


def normal_values(own_key, shape, deviation, reach, shards=(), kind=jnp.bfloat16):
    drawn = jax.random.normal(own_key, shape, jnp.float32) * deviation
    if len(shards) > 0:
        drawn = block_scale(own_key, shape, shards, -0.22, 0.18) * drawn
    return jnp.clip(drawn, min=-reach, max=reach).astype(kind)


def setup_inputs(seed: int = 0) -> dict:
    arg_keys = jax.random.split(jax.random.key(seed), 9)
    return {
        "grad_out": draw_grad_out(jax.random.fold_in(arg_keys[8], 71), 0),
        "context": draw_context(jax.random.fold_in(arg_keys[8], 71), 0),
        "weight": normal_values(arg_keys[2], (D, HD), D ** -0.5, 0.078125, ((1, 8),)),
        "master": normal_values(arg_keys[3], (D, HD), 0.1, 0.6, ((0, 16), (1, 8)), jnp.float32),
        "moment_q": normal_values(arg_keys[4], (D, HD), 150.0, 440.0, ((0, 16), (1, 8))),
        "second_moment": jnp.clip(jnp.exp(math.log(1.0) - 3.912023 * jax.random.uniform(arg_keys[5], (D, HD), jnp.float32) ** block_scale(arg_keys[5], (D, HD), ((0, 16), (1, 8)), -0.2, 0.2)), 0.02, 1.0),
        "moment_scale": jnp.clip(jax.random.uniform(arg_keys[6], (), jnp.float32, 300.0, 900.0), 300.0, 900.0),
        "scale_boost": jnp.clip(jax.random.uniform(arg_keys[7], (), jnp.float32, 1.25, 2.0), 1.25, 2.0),
    }


quant_top = 448.0
peak_eps = 1e-06
norm_eps = 1e-06
clip_rms = 0.5
beta_one = 0.9
beta_two = 0.95
bias_one = 1.0 - 0.9 ** 10
bias_two = 1.0 - 0.95 ** 10
adam_eps = 1e-08
rate_value = 0.01
decay_value = 0.1

def reference(grad_out, context, weight, master, moment_q, second_moment, moment_scale, scale_boost):
    input_grad = jnp.dot(grad_out, weight, preferred_element_type=jnp.float32).astype(jnp.bfloat16)
    rep_rows = TOK_DEV * N_MP

    def partial_sum(index):
        start = (index * rep_rows).astype(jnp.int32)
        rows_grad = lax.dynamic_slice_in_dim(grad_out, start, rep_rows, 0)
        rows_ctx = lax.dynamic_slice_in_dim(context, start, rep_rows, 0)
        return jnp.dot(rows_grad.T, rows_ctx, preferred_element_type=jnp.float32)

    def peak_step(best, index):
        return (jnp.maximum(best, jnp.max(jnp.abs(partial_sum(index)))), None)
    replicas = jnp.arange(N_DP, dtype=jnp.int32)
    peak, _ = lax.scan(peak_step, jnp.zeros((), jnp.float32), replicas)
    grad_scale = quant_top * scale_boost / (peak + peak_eps)

    def sum_step(total, index):
        scaled = jnp.clip(partial_sum(index) * grad_scale, -quant_top, quant_top)
        rounded = lax.optimization_barrier(scaled.astype(jnp.bfloat16))
        return (total + rounded.astype(jnp.float32), None)
    summed, _ = lax.scan(sum_step, jnp.zeros((D, HD), jnp.float32), replicas)
    gradient = summed / grad_scale
    norm_value = jnp.sqrt(jnp.sum(gradient * gradient) + norm_eps)
    clip_factor = clip_rms * math.sqrt(D * HD) / norm_value
    step_grad = clip_factor * gradient
    old_moment = moment_q.astype(jnp.float32) / moment_scale
    moment = beta_one * old_moment + (1.0 - beta_one) * step_grad
    new_second = beta_two * second_moment + (1.0 - beta_two) * step_grad * step_grad
    update = moment / bias_one / (jnp.sqrt(new_second / bias_two) + adam_eps) + decay_value * master
    new_master = master - rate_value * update
    new_scale = quant_top / (jnp.max(jnp.abs(moment)) + peak_eps)
    new_moment_q = (moment * new_scale).astype(jnp.bfloat16)
    new_weight = new_master.astype(jnp.bfloat16)
    return (input_grad, new_master, new_moment_q, new_second, new_scale, grad_scale, new_weight)
```

```python
import math

import jax
import jax.numpy as jnp
from jax import lax
from jax.sharding import PartitionSpec as P

D = 6144
HD = 6144
N_DEV = 128
LANES = 128


quant_top = 448.0
peak_eps = 1e-06
norm_eps = 1e-06
clip_rms = 0.5
beta_one = 0.9
beta_two = 0.95
bias_one = 1.0 - 0.9**10
bias_two = 1.0 - 0.95**10
adam_eps = 1e-08
rate_value = 0.01
decay_value = 0.1
contract_rows = (((0,), (0,)), ((), ()))


def input_product(full_grad, weight):
    return jnp.dot(full_grad, weight, preferred_element_type=jnp.float32).astype(jnp.bfloat16)


def spread(value):
    rows = jnp.broadcast_to(value, (N_DEV, LANES))
    return lax.all_to_all(rows, ("dp", "mp"), 0, 0, tiled=True)


def global_max(value):
    return jnp.max(spread(value))


def global_sum(value):
    return jnp.sum(spread(value)[:, 0])


def weight_gradient(full_grad, context, scale_boost):
    held = lax.dot_general(full_grad, context, contract_rows, preferred_element_type=jnp.float32)
    local_peak = jnp.max(jnp.abs(held))
    peak = global_max(local_peak)
    grad_scale = quant_top * scale_boost / (peak + peak_eps)
    scaled = held * grad_scale
    summed = lax.psum_scatter(
        jnp.clip(scaled, -quant_top, quant_top).astype(jnp.bfloat16),
        "dp",
        scatter_dimension=0,
        tiled=True,
    ).astype(jnp.float32)
    return (summed, grad_scale)


def local(grad_out, context, weight, master, moment_q, second_moment, moment_scale, scale_boost):
    full_grad = lax.all_gather(grad_out, "mp", axis=0, tiled=True)
    input_grad = input_product(full_grad, weight)
    summed, grad_scale = weight_gradient(full_grad, context, scale_boost)
    gradient = summed / grad_scale
    squares = global_sum(jnp.sum(gradient * gradient))
    norm_value = jnp.sqrt(squares + norm_eps)
    clip_factor = clip_rms * math.sqrt(D * HD) / norm_value
    step_grad = clip_factor * gradient
    old_moment = moment_q.astype(jnp.float32) / moment_scale
    moment = beta_one * old_moment + (1.0 - beta_one) * step_grad
    new_second = beta_two * second_moment + (1.0 - beta_two) * step_grad * step_grad
    update = moment / bias_one / (jnp.sqrt(new_second / bias_two) + adam_eps) + decay_value * master
    new_master = master - rate_value * update
    moment_top = global_max(jnp.max(jnp.abs(moment)))
    new_scale = quant_top / (moment_top + peak_eps)
    new_moment_q = (moment * new_scale).astype(jnp.bfloat16)
    new_weight = lax.all_gather(new_master.astype(jnp.bfloat16), "dp", axis=0, tiled=True)
    return (input_grad, new_master, new_moment_q, new_second, new_scale, grad_scale, new_weight)


def solution(mesh):
    return jax.shard_map(
        local,
        mesh=mesh,
        in_specs=(
            P(("dp", "mp"), None),
            P("dp", "mp"),
            P(None, "mp"),
            P("dp", "mp"),
            P("dp", "mp"),
            P("dp", "mp"),
            P(),
            P(),
        ),
        out_specs=(
            P("dp", "mp"),
            P("dp", "mp"),
            P("dp", "mp"),
            P("dp", "mp"),
            P(),
            P(),
            P(None, "mp"),
        ),
        check_vma=False,
    )
```

```python
import functools
import math

import jax
import jax.numpy as jnp
from jax import lax
from jax.experimental import pallas as pl
from jax.experimental.pallas import tpu as pltpu
from jax.sharding import Mesh
from jax.sharding import PartitionSpec as P

D = 6144
HD = 6144
N_DEV = 128
LANES = 128
SIDE = 4
STRIP = 384
SLAB = SIDE * STRIP
ROWS = 1024
TOK = 128
COLS = 768
MP = 8
WIDTH = 256
EVERY = ("y", "z", "x", "c")
MP_AXES = ("x", "c")


quant_top = 448.0
peak_eps = 1e-06
norm_eps = 1e-06
clip_rms = 0.5
beta_one = 0.9
beta_two = 0.95
bias_one = 1.0 - 0.9**10
bias_two = 1.0 - 0.95**10
adam_eps = 1e-08
rate_value = 0.01
decay_value = 0.1
contract_rows = (((0,), (0,)), ((), ()))


def exchange(rows):
    return lax.all_to_all(rows, EVERY, 0, 0, tiled=True)


def global_max(value):
    return jnp.max(exchange(jnp.broadcast_to(value, (N_DEV, LANES))))


def global_sum(value):
    return jnp.sum(exchange(jnp.broadcast_to(value, (N_DEV, LANES)))[:, 0])


def fetch(array, axis, step):
    size = lax.axis_size(axis)
    return lax.ppermute(array, axis, [((i + step) % size, i) for i in range(size)])


def keep(found, held, top):
    held[...] = found.astype(held.dtype).reshape(held.shape)
    most = jnp.max(jnp.abs(found), axis=0, keepdims=True)
    best = most[:, :LANES]
    for at in range(LANES, COLS, LANES):
        best = jnp.maximum(best, most[:, at : at + LANES])
    top[...] = jnp.maximum(top[...], best)


def product(rows, columns):
    return lax.dot_general(rows, columns, contract_rows, preferred_element_type=jnp.float32)


def own_kernel(places, mine, other, context, held, top, ordered):
    for at in range(MP):
        start = pl.multiple_of(places[at] * TOK, TOK)
        ordered[at * TOK : (at + 1) * TOK, :] = context[pl.ds(start, TOK), :]
    top[...] = jnp.zeros_like(top)
    half = ROWS // 2
    keep(product(mine[...], ordered[:half, :]) + product(other[...], ordered[half:, :]), held, top)


def own_partial(mine, other, context, places):
    return pl.pallas_call(
        own_kernel,
        in_specs=[pl.BlockSpec(memory_space=pltpu.SMEM)] + [pl.BlockSpec(memory_space=pltpu.VMEM)] * 3,
        out_specs=[pl.BlockSpec(memory_space=pltpu.VMEM)] * 2,
        out_shape=[
            jax.ShapeDtypeStruct((SLAB, COLS), jnp.bfloat16),
            jax.ShapeDtypeStruct((N_DEV, LANES), jnp.float32),
        ],
        scratch_shapes=[pltpu.VMEM((ROWS, COLS), jnp.bfloat16)],
        compiler_params=pltpu.CompilerParams(vmem_limit_bytes=60 * 2**20),
        cost_estimate=pl.CostEstimate(
            flops=2 * ROWS * SLAB * COLS,
            bytes_accessed=(ROWS * SLAB + ROWS * COLS + SLAB * COLS) * 2,
            transcendentals=0,
        ),
        name="own_partial",
    )(places, mine, other, context)


def partial_kernel(strips, above, below, upper, lower, held, top):
    which = pl.program_id(0)

    @pl.when(which == 0)
    def _():
        top[...] = jnp.zeros_like(top)

    for index, context in enumerate((above, below)):

        @pl.when(which == index)
        def _(context=context):
            keep(product(strips[...].reshape(ROWS, SLAB), context[...]), held, top)

    @pl.when(which == 2)
    def _():
        rows = strips[...].reshape(2, ROWS // 2, SLAB)
        keep(product(rows[0], upper[...]) + product(rows[1], lower[...]), held, top)


def partial_sums(strips, contexts):
    parts = SIDE - 1
    return pl.pallas_call(
        partial_kernel,
        grid=(parts,),
        in_specs=[pl.BlockSpec((MP, 1, TOK, SLAB), lambda k: (0, k, 0, 0))]
        + [pl.BlockSpec(held.shape, lambda k: (0, 0)) for held in contexts],
        out_specs=[
            pl.BlockSpec((1, SLAB, COLS), lambda k: (k, 0, 0)),
            pl.BlockSpec((N_DEV, LANES), lambda k: (0, 0)),
        ],
        out_shape=[
            jax.ShapeDtypeStruct((parts, SLAB, COLS), jnp.bfloat16),
            jax.ShapeDtypeStruct((N_DEV, LANES), jnp.float32),
        ],
        compiler_params=pltpu.CompilerParams(vmem_limit_bytes=60 * 2**20),
        cost_estimate=pl.CostEstimate(
            flops=2 * parts * ROWS * SLAB * COLS,
            bytes_accessed=parts * (ROWS * SLAB + ROWS * COLS + SLAB * COLS) * 2,
            transcendentals=0,
        ),
        name="partial_sums",
    )(strips, *contexts)


def input_kernel(count, starts, weight, *refs):
    pieces, out, whole, arrived = refs[:count], refs[count], refs[count + 1], refs[count + 2]

    @pl.when(pl.program_id(0) == 0)
    def _():
        copies = []
        for at, piece in enumerate(pieces):
            rows = piece.shape[0]
            start = pl.multiple_of(starts[at], TOK // 2)
            copies.append(pltpu.make_async_copy(piece, whole.at[pl.ds(start, rows), :], arrived.at[at]))
        for copy in copies:
            copy.start()
        for copy in copies:
            copy.wait()

    found = jnp.dot(whole[...], weight[...], preferred_element_type=jnp.float32)
    out[...] = found.astype(out.dtype)


def input_product(pieces, starts, weight):
    count = len(pieces)
    return pl.pallas_call(
        functools.partial(input_kernel, count),
        grid_spec=pltpu.PrefetchScalarGridSpec(
            num_scalar_prefetch=1,
            grid=(COLS // WIDTH,),
            in_specs=[pl.BlockSpec((D, WIDTH), lambda n, at: (0, n))]
            + [pl.BlockSpec(memory_space=pl.ANY)] * count,
            out_specs=pl.BlockSpec((ROWS, WIDTH), lambda n, at: (0, n)),
            scratch_shapes=[pltpu.VMEM((ROWS, D), jnp.bfloat16), pltpu.SemaphoreType.DMA((count,))],
        ),
        out_shape=jax.ShapeDtypeStruct((ROWS, COLS), jnp.bfloat16),
        compiler_params=pltpu.CompilerParams(vmem_limit_bytes=60 * 2**20),
        cost_estimate=pl.CostEstimate(
            flops=2 * ROWS * D * COLS,
            bytes_accessed=(ROWS * D + D * COLS + ROWS * COLS) * 2,
            transcendentals=0,
        ),
        name="input_product",
    )(starts, weight, *pieces)


def neighbours(array, axis):
    return fetch(array, axis, 1), fetch(array, axis, -1)


def opposite(ahead, behind, axis):
    half = ahead.shape[0] // 2
    return fetch(ahead[:half], axis, 1), fetch(behind[half:], axis, -1)


def adam_step(gradient, clip_factor, master, moment_q, second_moment, moment_scale):
    step_grad = clip_factor * gradient
    old_moment = moment_q.astype(jnp.float32) / moment_scale
    moment = beta_one * old_moment + (1.0 - beta_one) * step_grad
    new_second = beta_two * second_moment + (1.0 - beta_two) * step_grad * step_grad
    update = moment / bias_one / (jnp.sqrt(new_second / bias_two) + adam_eps) + decay_value * master
    return moment, new_second, master - rate_value * update


def local(grad_out, context, weight, master, moment_q, second_moment, moment_scale, scale_boost):
    row, column, core = lax.axis_index("y"), lax.axis_index("x"), lax.axis_index("c")
    own = lax.dynamic_slice(grad_out, (0, row * SLAB), (TOK, SLAB))
    blocks = [own] + [fetch(own, "x", step) for step in (1, 3, 2)]
    strips = jnp.stack([grad_out[:, at : at + SLAB] for at in range(0, D, SLAB)])
    strips = lax.all_to_all(strips, "y", 0, 0, tiled=True)
    source, strips, blocks = lax.optimization_barrier((context, strips, blocks))
    strips = jnp.concatenate(
        [lax.dynamic_slice(strips, (lax.rem(row + step, SIDE), 0, 0), (1, TOK, SLAB)) for step in (1, 3, 2)]
    )
    slabs = lax.all_gather(strips, MP_AXES, axis=0, tiled=True).reshape(MP, SIDE - 1, TOK, SLAB)
    above, below = neighbours(source, "y")
    upper, lower = opposite(above, below, "y")
    mine = jnp.concatenate(blocks)
    chips = lax.rem(column + jnp.array((0, 1, 3, 2), jnp.int32), SIDE) * 2
    held_own, top_own = own_partial(mine, fetch(mine, "c", 1), context, jnp.concatenate([chips + core, chips + 1 - core]))
    held, top = partial_sums(slabs, (above, below, upper, lower))
    top = jnp.maximum(top, top_own)
    peak = jnp.max(exchange(top))
    grad_scale = quant_top * scale_boost / (peak + peak_eps)
    total = jnp.zeros((SLAB, COLS), jnp.float32)
    for part in (held_own, held[0], held[1], held[2]):
        total = total + jnp.clip(part.astype(jnp.float32) * grad_scale, -quant_top, quant_top)
    half = TOK // 2
    early, late = grad_out[:half], grad_out[half:]
    total, early, late = lax.optimization_barrier((total.astype(jnp.bfloat16), early, late))
    summed = lax.psum_scatter(total, "z", scatter_dimension=0, tiled=True)
    ahead_early, behind_late = fetch(early, "x", 1), fetch(late, "x", -1)
    summed, ahead_early, behind_late = lax.optimization_barrier((summed, ahead_early, behind_late))
    summed = summed.astype(jnp.float32)
    gradient = summed / grad_scale
    squares = global_sum(jnp.sum(gradient * gradient))
    norm_value = jnp.sqrt(squares + norm_eps)
    clip_factor = clip_rms * math.sqrt(D * HD) / norm_value
    _, _, new_master = adam_step(gradient, clip_factor, master, moment_q, second_moment, moment_scale)
    shard = new_master.astype(jnp.bfloat16)
    (
        shard,
        early,
        late,
        ahead_early,
        behind_late,
        gradient,
        master,
        moment_q,
        second_moment,
    ) = lax.optimization_barrier(
        (shard, early, late, ahead_early, behind_late, gradient, master, moment_q, second_moment)
    )
    new_weight = lax.all_gather(shard, ("y", "z"), axis=0, tiled=True)
    moment, new_second, new_master = adam_step(gradient, clip_factor, master, moment_q, second_moment, moment_scale)
    moment_top = global_max(jnp.max(jnp.abs(moment)))
    new_scale = quant_top / (moment_top + peak_eps)
    new_moment_q = (moment * new_scale).astype(jnp.bfloat16)
    ahead_late, behind_early = fetch(late, "x", 1), fetch(early, "x", -1)
    far_early, far_late = fetch(ahead_early, "x", 1), fetch(behind_late, "x", -1)
    found = (
        (0, 0, grad_out),
        (1, 0, ahead_early),
        (3, half, behind_late),
        (1, half, ahead_late),
        (3, 0, behind_early),
        (2, 0, far_early),
        (2, half, far_late),
    )
    pieces, starts = [], []
    for step, start, piece in found:
        chip = lax.rem(column + step, SIDE) * 2
        pieces += [piece, fetch(piece, "c", 1)]
        starts += [(chip + core) * TOK + start, (chip + 1 - core) * TOK + start]
    input_grad = input_product(pieces, jnp.stack(starts), weight)
    return (input_grad, new_master, new_moment_q, new_second, new_scale, grad_scale, new_weight)


def solution(mesh):
    fine = Mesh(mesh.devices.reshape(SIDE, SIDE, SIDE, 2), EVERY)
    dp, mp = ("y", "z"), MP_AXES
    return jax.shard_map(
        local,
        mesh=fine,
        in_specs=(
            P(dp + mp, None),
            P(dp, mp),
            P(None, mp),
            P(dp, mp),
            P(dp, mp),
            P(dp, mp),
            P(),
            P(),
        ),
        out_specs=(
            P(dp, mp),
            P(dp, mp),
            P(dp, mp),
            P(dp, mp),
            P(),
            P(),
            P(None, mp),
        ),
        check_vma=False,
    )
```

```python
import functools
import math

import jax
import jax.numpy as jnp
from jax import lax
from jax.experimental import pallas as pl
from jax.experimental.pallas import tpu as pltpu
from jax.sharding import Mesh
from jax.sharding import PartitionSpec as P

D = 6144
HD = 6144
N_DEV = 128
LANES = 128
SIDE = 4
STRIP = 384
SLAB = SIDE * STRIP
ROWS = 1024
TOK = 128
COLS = 768
MP = 8
WIDTH = 256
EVERY = ("y", "z", "x", "c")
MP_AXES = ("x", "c")


quant_top = 448.0
peak_eps = 1e-06
norm_eps = 1e-06
clip_rms = 0.5
beta_one = 0.9
beta_two = 0.95
bias_one = 1.0 - 0.9**10
bias_two = 1.0 - 0.95**10
adam_eps = 1e-08
rate_value = 0.01
decay_value = 0.1
contract_rows = (((0,), (0,)), ((), ()))


def exchange(rows):
    return lax.all_to_all(rows, EVERY, 0, 0, tiled=True)


def fetch(array, axis, step):
    size = lax.axis_size(axis)
    return lax.ppermute(array, axis, [((i + step) % size, i) for i in range(size)])


def keep(found, held, top):
    held[...] = found.astype(held.dtype).reshape(held.shape)
    most = jnp.max(jnp.abs(found), axis=0, keepdims=True)
    best = most[:, :LANES]
    for at in range(LANES, COLS, LANES):
        best = jnp.maximum(best, most[:, at : at + LANES])
    top[...] = jnp.maximum(top[...], best)


def product(rows, columns):
    return lax.dot_general(rows, columns, contract_rows, preferred_element_type=jnp.float32)


def blocks_kernel(count, places, mine, other, *refs):
    contexts, first_top, held, top, ordered = refs[:count], *refs[count:]
    share = MP // count

    @pl.when(pl.program_id(0) == 0)
    def _():
        top[...] = first_top[...]
        for at in range(MP):
            place = places[at]
            for index, context in enumerate(contexts):

                @pl.when(place // share == index)
                def _(at=at, place=place, index=index, context=context):
                    start = pl.multiple_of((place - index * share) * TOK, TOK)
                    ordered[at * TOK : (at + 1) * TOK, :] = context[pl.ds(start, TOK), :]

    half = ROWS // 2
    keep(product(mine[...], ordered[:half, :]) + product(other[...], ordered[half:, :]), held, top)


def blocks_partial(mine, other, contexts, places, top):
    count = len(contexts)
    tile = 512
    strip = pl.BlockSpec((ROWS // 2, tile), lambda i: (0, i))
    return pl.pallas_call(
        functools.partial(blocks_kernel, count),
        grid=(SLAB // tile,),
        in_specs=[pl.BlockSpec(memory_space=pltpu.SMEM), strip, strip]
        + [pl.BlockSpec(held.shape, lambda i: (0, 0)) for held in (*contexts, top)],
        out_specs=[pl.BlockSpec((tile, COLS), lambda i: (i, 0)), pl.BlockSpec((N_DEV, LANES), lambda i: (0, 0))],
        out_shape=[
            jax.ShapeDtypeStruct((SLAB, COLS), jnp.bfloat16),
            jax.ShapeDtypeStruct((N_DEV, LANES), jnp.float32),
        ],
        scratch_shapes=[pltpu.VMEM((ROWS, COLS), jnp.bfloat16)],
        compiler_params=pltpu.CompilerParams(vmem_limit_bytes=60 * 2**20),
        cost_estimate=pl.CostEstimate(
            flops=2 * ROWS * SLAB * COLS,
            bytes_accessed=(ROWS * SLAB + ROWS * COLS + SLAB * COLS) * 2,
            transcendentals=0,
        ),
        name="blocks_partial",
    )(places, mine, other, *contexts, top)


def partial_kernel(strips, above, below, first_top, held, top):
    which = pl.program_id(0)

    @pl.when(which == 0)
    def _():
        top[...] = first_top[...]

    for index, context in enumerate((above, below)):

        @pl.when(which == index)
        def _(context=context):
            keep(product(strips[...].reshape(ROWS, SLAB), context[...]), held, top)


def partial_sums(strips, contexts, top):
    parts = len(contexts)
    return pl.pallas_call(
        partial_kernel,
        grid=(parts,),
        in_specs=[pl.BlockSpec((MP, 1, TOK, SLAB), lambda k: (0, k, 0, 0))]
        + [pl.BlockSpec(held.shape, lambda k: (0, 0)) for held in (*contexts, top)],
        out_specs=[
            pl.BlockSpec((1, SLAB, COLS), lambda k: (k, 0, 0)),
            pl.BlockSpec((N_DEV, LANES), lambda k: (0, 0)),
        ],
        out_shape=[
            jax.ShapeDtypeStruct((parts, SLAB, COLS), jnp.bfloat16),
            jax.ShapeDtypeStruct((N_DEV, LANES), jnp.float32),
        ],
        compiler_params=pltpu.CompilerParams(vmem_limit_bytes=60 * 2**20),
        cost_estimate=pl.CostEstimate(
            flops=2 * parts * ROWS * SLAB * COLS,
            bytes_accessed=parts * (ROWS * SLAB + ROWS * COLS + SLAB * COLS) * 2,
            transcendentals=0,
        ),
        name="partial_sums",
    )(strips, *contexts, top)


def square_kernel(scale, summed, sums):
    gradient = summed[...].astype(jnp.float32) / scale[0]
    found = jnp.sum(gradient * gradient, axis=0, keepdims=True)
    lanes = found[:, :LANES]
    for at in range(LANES, COLS, LANES):
        lanes = lanes + found[:, at : at + LANES]
    sums[...] = jnp.broadcast_to(lanes, sums.shape)


def square_sums(summed, scale):
    return pl.pallas_call(
        square_kernel,
        in_specs=[pl.BlockSpec(memory_space=pltpu.SMEM), pl.BlockSpec(memory_space=pltpu.VMEM)],
        out_shape=jax.ShapeDtypeStruct((N_DEV, LANES), jnp.float32),
        compiler_params=pltpu.CompilerParams(vmem_limit_bytes=60 * 2**20),
        name="square_sums",
    )(scale.reshape(1), summed)


def input_kernel(sizes, starts, weight, *refs):
    count = len(sizes)
    pieces, out, whole, held, arrived, left = refs[:count], *refs[-5:]
    step, steps = pl.program_id(0), COLS // WIDTH

    @pl.when(step == 0)
    def _():
        copies, offset = [], 0
        for at, piece in enumerate(pieces):
            copies.append(pltpu.make_async_copy(piece, whole.at[offset : offset + sizes[at], :], arrived.at[at]))
            offset += sizes[at]
        for copy in copies:
            copy.start()
        for copy in copies:
            copy.wait()

    found = jnp.dot(whole[...], weight[...], preferred_element_type=jnp.float32)
    for index in range(steps):

        @pl.when(step == index)
        def _(index=index):
            held[:, index * WIDTH : (index + 1) * WIDTH] = found.astype(held.dtype)

    @pl.when(step == steps - 1)
    def _():
        copies, offset = [], 0
        for at in range(count):
            start = pl.multiple_of(starts[at], TOK // 2)
            copies.append(
                pltpu.make_async_copy(
                    held.at[offset : offset + sizes[at], :], out.at[pl.ds(start, sizes[at]), :], left.at[at]
                )
            )
            offset += sizes[at]
        for copy in copies:
            copy.start()
        for copy in copies:
            copy.wait()


def input_product(pieces, starts, weight, before=None):
    count = len(pieces)
    sizes = tuple(piece.shape[0] for piece in pieces)
    operands = [jnp.stack(starts), weight, *pieces]
    anywhere = pl.BlockSpec(memory_space=pl.ANY)
    in_specs = [pl.BlockSpec((D, WIDTH), lambda n, at: (0, n))] + [anywhere] * count
    aliases = {}
    if before is not None:
        aliases = {len(operands): 0}
        operands.append(before)
        in_specs.append(anywhere)
    return pl.pallas_call(
        functools.partial(input_kernel, sizes),
        grid_spec=pltpu.PrefetchScalarGridSpec(
            num_scalar_prefetch=1,
            grid=(COLS // WIDTH,),
            in_specs=in_specs,
            out_specs=anywhere,
            scratch_shapes=[
                pltpu.VMEM((sum(sizes), D), jnp.bfloat16),
                pltpu.VMEM((sum(sizes), COLS), jnp.bfloat16),
                pltpu.SemaphoreType.DMA((count,)),
                pltpu.SemaphoreType.DMA((count,)),
            ],
        ),
        out_shape=jax.ShapeDtypeStruct((ROWS, COLS), jnp.bfloat16),
        input_output_aliases=aliases,
        compiler_params=pltpu.CompilerParams(vmem_limit_bytes=60 * 2**20),
        cost_estimate=pl.CostEstimate(
            flops=2 * sum(sizes) * D * COLS,
            bytes_accessed=(sum(sizes) * D + D * COLS + sum(sizes) * COLS) * 2,
            transcendentals=0,
        ),
        name="input_product",
    )(*operands)


def neighbours(array, axis):
    return fetch(array, axis, 1), fetch(array, axis, -1)


def opposite(ahead, behind, axis):
    half = ahead.shape[0] // 2
    return fetch(ahead[:half], axis, 1), fetch(behind[half:], axis, -1)


def adam_step(gradient, clip_factor, master, moment_q, second_moment, moment_scale):
    step_grad = clip_factor * gradient
    old_moment = moment_q.astype(jnp.float32) / moment_scale
    moment = beta_one * old_moment + (1.0 - beta_one) * step_grad
    new_second = beta_two * second_moment + (1.0 - beta_two) * step_grad * step_grad
    update = moment / bias_one / (jnp.sqrt(new_second / bias_two) + adam_eps) + decay_value * master
    return moment, new_second, master - rate_value * update


def local(grad_out, context, weight, master, moment_q, second_moment, moment_scale, scale_boost):
    row, column, core = lax.axis_index("y"), lax.axis_index("x"), lax.axis_index("c")

    def strip(step):
        return lax.dynamic_slice(grad_out, (0, lax.rem(row + step, SIDE) * SLAB), (TOK, SLAB))

    own = strip(0)
    strips = jnp.stack([fetch(strip(3), "y", 1), fetch(strip(1), "y", -1)])
    own_ahead, own_behind = neighbours(own, "x")
    strips, own_ahead, own_behind, own_again, far = lax.optimization_barrier(
        (strips, own_ahead, own_behind, own, strip(2))
    )
    slabs = lax.all_gather(strips, MP_AXES, axis=0, tiled=True).reshape(MP, 2, TOK, SLAB)
    own_far = fetch(own_again, "x", 2)
    far = fetch(far, "y", 2)
    source, own_far, far = lax.optimization_barrier((context, own_far, far))
    above, below = neighbours(source, "y")
    far_ahead, far_behind = neighbours(far, "x")
    upper, lower = opposite(above, below, "y")
    chips = lax.rem(column + jnp.array((0, 1, 3, 2), jnp.int32), SIDE) * 2
    places = jnp.concatenate([chips + core, chips + 1 - core])
    mine = jnp.concatenate([own, own_ahead, own_behind, own_far])
    nothing = jnp.zeros((N_DEV, LANES), jnp.float32)
    held_own, top = blocks_partial(mine, fetch(mine, "c", 1), (context,), places, nothing)
    far, top = lax.optimization_barrier((far, top))
    far_far = fetch(far, "x", 2)
    held, top = partial_sums(slabs, (above, below), top)
    mine = jnp.concatenate([far, far_ahead, far_behind, far_far])
    held_far, top = blocks_partial(mine, fetch(mine, "c", 1), (upper, lower), places, top)
    peak = jnp.max(exchange(top))
    grad_scale = quant_top * scale_boost / (peak + peak_eps)
    limit = quant_top / grad_scale
    total = jnp.zeros((SLAB, COLS), jnp.float32)
    for part in (held_own, held[0], held[1], held_far):
        total = total + jnp.clip(part.astype(jnp.float32), -limit, limit)
    total = (total * grad_scale).astype(jnp.bfloat16)
    half = TOK // 2
    early, late = grad_out[:half], grad_out[half:]
    total, early, late = lax.optimization_barrier((total, early, late))
    summed = lax.psum_scatter(total, "z", scatter_dimension=0, tiled=True)
    ahead_early, behind_late = fetch(early, "x", 1), fetch(late, "x", -1)
    summed, ahead_early, behind_late = lax.optimization_barrier((summed, ahead_early, behind_late))
    squares = jnp.sum(exchange(square_sums(summed, grad_scale)))
    clip_factor = clip_rms * math.sqrt(D * HD) / jnp.sqrt(squares + norm_eps)
    gradient = summed.astype(jnp.float32) / grad_scale
    _, _, new_master = adam_step(gradient, clip_factor, master, moment_q, second_moment, moment_scale)
    shard = new_master.astype(jnp.bfloat16)
    shard, early, late, ahead_early, behind_late, summed = lax.optimization_barrier(
        (shard, early, late, ahead_early, behind_late, summed)
    )
    new_weight = lax.all_gather(shard, ("y", "z"), axis=0, tiled=True)
    gradient = summed.astype(jnp.float32) / grad_scale
    moment, new_second, new_master = adam_step(gradient, clip_factor, master, moment_q, second_moment, moment_scale)
    ahead_late, behind_early = fetch(late, "x", 1), fetch(early, "x", -1)

    def gathered(group, before):
        pieces, starts = [], []
        for step, start, piece in group:
            chip = lax.rem(column + step, SIDE) * 2
            pieces += [piece, fetch(piece, "c", 1)]
            starts += [(chip + core) * TOK + start, (chip + 1 - core) * TOK + start]
        return input_product(pieces, starts, weight, before)

    input_grad = gathered(((0, 0, grad_out), (1, 0, ahead_early), (3, half, behind_late)), None)
    ahead_early, behind_late, input_grad = lax.optimization_barrier((ahead_early, behind_late, input_grad))
    far_early, far_late = fetch(ahead_early, "x", 1), fetch(behind_late, "x", -1)
    moment, far_early, far_late = lax.optimization_barrier((moment, far_early, far_late))
    moment_tops = exchange(jnp.broadcast_to(jnp.max(jnp.abs(moment)), (N_DEV, LANES)))
    others = ((1, half, ahead_late), (3, 0, behind_early), (2, 0, far_early), (2, half, far_late))
    input_grad = gathered(others, input_grad)
    moment_tops, input_grad = lax.optimization_barrier((moment_tops, input_grad))
    new_scale = quant_top / (jnp.max(moment_tops) + peak_eps)
    new_moment_q = (moment * new_scale).astype(jnp.bfloat16)
    return (input_grad, new_master, new_moment_q, new_second, new_scale, grad_scale, new_weight)


def solution(mesh):
    fine = Mesh(mesh.devices.reshape(SIDE, SIDE, SIDE, 2), EVERY)
    dp, mp = ("y", "z"), MP_AXES
    return jax.shard_map(
        local,
        mesh=fine,
        in_specs=(
            P(dp + mp, None),
            P(dp, mp),
            P(None, mp),
            P(dp, mp),
            P(dp, mp),
            P(dp, mp),
            P(),
            P(),
        ),
        out_specs=(
            P(dp, mp),
            P(dp, mp),
            P(dp, mp),
            P(dp, mp),
            P(),
            P(),
            P(None, mp),
        ),
        check_vma=False,
    )
```

```python
import functools
import math

import jax
import jax.numpy as jnp
from jax import lax
from jax.experimental import pallas as pl
from jax.experimental.pallas import tpu as pltpu
from jax.sharding import Mesh
from jax.sharding import PartitionSpec as P

D = 6144
HD = 6144
N_DEV = 128
LANES = 128
SIDE = 4
STRIP = 384
SLAB = SIDE * STRIP
ROWS = 1024
TOK = 128
COLS = 768
MP = 8
WIDTH = 256
EVERY = ("y", "z", "x", "c")
MP_AXES = ("x", "c")


quant_top = 448.0
peak_eps = 1e-06
norm_eps = 1e-06
clip_rms = 0.5
beta_one = 0.9
beta_two = 0.95
bias_one = 1.0 - 0.9**10
bias_two = 1.0 - 0.95**10
adam_eps = 1e-08
rate_value = 0.01
decay_value = 0.1
contract_rows = (((0,), (0,)), ((), ()))


def exchange(rows):
    return lax.all_to_all(rows, EVERY, 0, 0, tiled=True)


def fetch(array, axis, step):
    size = lax.axis_size(axis)
    return lax.ppermute(array, axis, [((i + step) % size, i) for i in range(size)])


def keep(found, held, top):
    held[...] = found.astype(held.dtype).reshape(held.shape)
    most = jnp.max(jnp.abs(found), axis=0, keepdims=True)
    best = most[:, :LANES]
    for at in range(LANES, COLS, LANES):
        best = jnp.maximum(best, most[:, at : at + LANES])
    top[...] = jnp.maximum(top[...], best)


def product(rows, columns):
    return lax.dot_general(rows, columns, contract_rows, preferred_element_type=jnp.float32)


def blocks_kernel(count, places, mine, other, *refs):
    contexts, first_top, held, top, ordered = refs[:count], *refs[count:]
    share = MP // count

    @pl.when(pl.program_id(0) == 0)
    def _():
        top[...] = first_top[...]
        for at in range(MP):
            place = places[at]
            for index, context in enumerate(contexts):

                @pl.when(place // share == index)
                def _(at=at, place=place, index=index, context=context):
                    start = pl.multiple_of((place - index * share) * TOK, TOK)
                    ordered[at * TOK : (at + 1) * TOK, :] = context[pl.ds(start, TOK), :]

    half = ROWS // 2
    keep(product(mine[...], ordered[:half, :]) + product(other[...], ordered[half:, :]), held, top)


def blocks_partial(mine, other, contexts, places, top):
    count = len(contexts)
    tile = 768
    strip = pl.BlockSpec((ROWS // 2, tile), lambda i: (0, i))
    return pl.pallas_call(
        functools.partial(blocks_kernel, count),
        grid=(SLAB // tile,),
        in_specs=[pl.BlockSpec(memory_space=pltpu.SMEM), strip, strip]
        + [pl.BlockSpec(held.shape, lambda i: (0, 0)) for held in (*contexts, top)],
        out_specs=[pl.BlockSpec((tile, COLS), lambda i: (i, 0)), pl.BlockSpec((N_DEV, LANES), lambda i: (0, 0))],
        out_shape=[
            jax.ShapeDtypeStruct((SLAB, COLS), jnp.bfloat16),
            jax.ShapeDtypeStruct((N_DEV, LANES), jnp.float32),
        ],
        scratch_shapes=[pltpu.VMEM((ROWS, COLS), jnp.bfloat16)],
        compiler_params=pltpu.CompilerParams(vmem_limit_bytes=60 * 2**20),
        cost_estimate=pl.CostEstimate(
            flops=2 * ROWS * SLAB * COLS,
            bytes_accessed=(ROWS * SLAB + ROWS * COLS + SLAB * COLS) * 2,
            transcendentals=0,
        ),
        name="blocks_partial",
    )(places, mine, other, *contexts, top)


def partial_kernel(strips, above, below, first_top, held, top):
    which = pl.program_id(0)

    @pl.when(which == 0)
    def _():
        top[...] = first_top[...]

    for index, context in enumerate((above, below)):

        @pl.when(which == index)
        def _(context=context):
            keep(product(strips[...].reshape(ROWS, SLAB), context[...]), held, top)


def partial_sums(strips, contexts, top):
    parts = len(contexts)
    return pl.pallas_call(
        partial_kernel,
        grid=(parts,),
        in_specs=[pl.BlockSpec((MP, 1, TOK, SLAB), lambda k: (0, k, 0, 0))]
        + [pl.BlockSpec(held.shape, lambda k: (0, 0)) for held in (*contexts, top)],
        out_specs=[
            pl.BlockSpec((1, SLAB, COLS), lambda k: (k, 0, 0)),
            pl.BlockSpec((N_DEV, LANES), lambda k: (0, 0)),
        ],
        out_shape=[
            jax.ShapeDtypeStruct((parts, SLAB, COLS), jnp.bfloat16),
            jax.ShapeDtypeStruct((N_DEV, LANES), jnp.float32),
        ],
        compiler_params=pltpu.CompilerParams(vmem_limit_bytes=60 * 2**20),
        cost_estimate=pl.CostEstimate(
            flops=2 * parts * ROWS * SLAB * COLS,
            bytes_accessed=parts * (ROWS * SLAB + ROWS * COLS + SLAB * COLS) * 2,
            transcendentals=0,
        ),
        name="partial_sums",
    )(strips, *contexts, top)


def square_kernel(scale, summed, sums):
    gradient = summed[...].astype(jnp.float32) / scale[0]
    found = jnp.sum(gradient * gradient, axis=0, keepdims=True)
    lanes = found[:, :LANES]
    for at in range(LANES, COLS, LANES):
        lanes = lanes + found[:, at : at + LANES]
    sums[...] = jnp.broadcast_to(lanes, sums.shape)


def square_sums(summed, scale):
    return pl.pallas_call(
        square_kernel,
        in_specs=[pl.BlockSpec(memory_space=pltpu.SMEM), pl.BlockSpec(memory_space=pltpu.VMEM)],
        out_shape=jax.ShapeDtypeStruct((N_DEV, LANES), jnp.float32),
        compiler_params=pltpu.CompilerParams(vmem_limit_bytes=60 * 2**20),
        name="square_sums",
    )(scale.reshape(1), summed)


def input_kernel(sizes, starts, weight, *refs):
    count = len(sizes)
    pieces, out, whole, held, arrived, left = refs[:count], *refs[-5:]
    step, steps = pl.program_id(0), COLS // WIDTH

    @pl.when(step == 0)
    def _():
        copies, offset = [], 0
        for at, piece in enumerate(pieces):
            copies.append(pltpu.make_async_copy(piece, whole.at[offset : offset + sizes[at], :], arrived.at[at]))
            offset += sizes[at]
        for copy in copies:
            copy.start()
        for copy in copies:
            copy.wait()

    found = jnp.dot(whole[...], weight[...], preferred_element_type=jnp.float32)
    for index in range(steps):

        @pl.when(step == index)
        def _(index=index):
            held[:, index * WIDTH : (index + 1) * WIDTH] = found.astype(held.dtype)

    @pl.when(step == steps - 1)
    def _():
        copies, offset = [], 0
        for at in range(count):
            start = pl.multiple_of(starts[at], TOK // 2)
            copies.append(
                pltpu.make_async_copy(
                    held.at[offset : offset + sizes[at], :], out.at[pl.ds(start, sizes[at]), :], left.at[at]
                )
            )
            offset += sizes[at]
        for copy in copies:
            copy.start()
        for copy in copies:
            copy.wait()


def input_product(pieces, starts, weight, before=None):
    count = len(pieces)
    sizes = tuple(piece.shape[0] for piece in pieces)
    operands = [jnp.stack(starts), weight, *pieces]
    anywhere = pl.BlockSpec(memory_space=pl.ANY)
    in_specs = [pl.BlockSpec((D, WIDTH), lambda n, at: (0, n))] + [anywhere] * count
    aliases = {}
    if before is not None:
        aliases = {len(operands): 0}
        operands.append(before)
        in_specs.append(anywhere)
    return pl.pallas_call(
        functools.partial(input_kernel, sizes),
        grid_spec=pltpu.PrefetchScalarGridSpec(
            num_scalar_prefetch=1,
            grid=(COLS // WIDTH,),
            in_specs=in_specs,
            out_specs=anywhere,
            scratch_shapes=[
                pltpu.VMEM((sum(sizes), D), jnp.bfloat16),
                pltpu.VMEM((sum(sizes), COLS), jnp.bfloat16),
                pltpu.SemaphoreType.DMA((count,)),
                pltpu.SemaphoreType.DMA((count,)),
            ],
        ),
        out_shape=jax.ShapeDtypeStruct((ROWS, COLS), jnp.bfloat16),
        input_output_aliases=aliases,
        compiler_params=pltpu.CompilerParams(vmem_limit_bytes=60 * 2**20),
        cost_estimate=pl.CostEstimate(
            flops=2 * sum(sizes) * D * COLS,
            bytes_accessed=(sum(sizes) * D + D * COLS + sum(sizes) * COLS) * 2,
            transcendentals=0,
        ),
        name="input_product",
    )(*operands)


def neighbours(array, axis):
    return fetch(array, axis, 1), fetch(array, axis, -1)


def opposite(ahead, behind, axis):
    half = ahead.shape[0] // 2
    return fetch(ahead[:half], axis, 1), fetch(behind[half:], axis, -1)


def adam_step(gradient, clip_factor, master, moment_q, second_moment, moment_scale):
    step_grad = clip_factor * gradient
    old_moment = moment_q.astype(jnp.float32) / moment_scale
    moment = beta_one * old_moment + (1.0 - beta_one) * step_grad
    new_second = beta_two * second_moment + (1.0 - beta_two) * step_grad * step_grad
    update = moment / bias_one / (jnp.sqrt(new_second / bias_two) + adam_eps) + decay_value * master
    return moment, new_second, master - rate_value * update


def local(grad_out, context, weight, master, moment_q, second_moment, moment_scale, scale_boost):
    row, column, core = lax.axis_index("y"), lax.axis_index("x"), lax.axis_index("c")

    def strip(step):
        return lax.dynamic_slice(grad_out, (0, lax.rem(row + step, SIDE) * SLAB), (TOK, SLAB))

    own = strip(0)
    strips = jnp.stack([fetch(strip(3), "y", 1), fetch(strip(1), "y", -1)])
    own_ahead, own_behind = neighbours(own, "x")
    strips, own_ahead, own_behind, own_again, far = lax.optimization_barrier(
        (strips, own_ahead, own_behind, own, strip(2))
    )
    slabs = lax.all_gather(strips, MP_AXES, axis=0, tiled=True).reshape(MP, 2, TOK, SLAB)
    own_far = fetch(own_again, "x", 2)
    far = fetch(far, "y", 2)
    source, own_far, far = lax.optimization_barrier((context, own_far, far))
    above, below = neighbours(source, "y")
    far_ahead, far_behind = neighbours(far, "x")
    upper, lower = opposite(above, below, "y")
    chips = lax.rem(column + jnp.array((0, 1, 3, 2), jnp.int32), SIDE) * 2
    places = jnp.concatenate([chips + core, chips + 1 - core])
    mine = jnp.concatenate([own, own_ahead, own_behind, own_far])
    nothing = jnp.zeros((N_DEV, LANES), jnp.float32)
    held_own, top = blocks_partial(mine, fetch(mine, "c", 1), (context,), places, nothing)
    far, top = lax.optimization_barrier((far, top))
    far_far = fetch(far, "x", 2)
    held, top = partial_sums(slabs, (above, below), top)
    mine = jnp.concatenate([far, far_ahead, far_behind, far_far])
    held_far, top = blocks_partial(mine, fetch(mine, "c", 1), (upper, lower), places, top)
    peak = jnp.max(exchange(top))
    grad_scale = quant_top * scale_boost / (peak + peak_eps)
    limit = quant_top / grad_scale
    total = jnp.zeros((SLAB, COLS), jnp.float32)
    for part in (held_own, held[0], held[1], held_far):
        total = total + jnp.clip(part.astype(jnp.float32), -limit, limit)
    total = (total * grad_scale).astype(jnp.bfloat16)
    half = TOK // 2
    early, late = grad_out[:half], grad_out[half:]
    total, early, late = lax.optimization_barrier((total, early, late))
    summed = lax.psum_scatter(total, "z", scatter_dimension=0, tiled=True)
    ahead_early, behind_late = fetch(early, "x", 1), fetch(late, "x", -1)
    summed, ahead_early, behind_late = lax.optimization_barrier((summed, ahead_early, behind_late))
    squares = jnp.sum(exchange(square_sums(summed, grad_scale)))
    clip_factor = clip_rms * math.sqrt(D * HD) / jnp.sqrt(squares + norm_eps)
    gradient = summed.astype(jnp.float32) / grad_scale
    _, _, new_master = adam_step(gradient, clip_factor, master, moment_q, second_moment, moment_scale)
    shard = new_master.astype(jnp.bfloat16)
    shard, early, late, ahead_early, behind_late, summed = lax.optimization_barrier(
        (shard, early, late, ahead_early, behind_late, summed)
    )
    new_weight = lax.all_gather(shard, ("y", "z"), axis=0, tiled=True)
    gradient = summed.astype(jnp.float32) / grad_scale
    moment, new_second, new_master = adam_step(gradient, clip_factor, master, moment_q, second_moment, moment_scale)
    ahead_late, behind_early = fetch(late, "x", 1), fetch(early, "x", -1)

    def gathered(group, before):
        pieces, starts = [], []
        for step, start, piece in group:
            chip = lax.rem(column + step, SIDE) * 2
            pieces += [piece, fetch(piece, "c", 1)]
            starts += [(chip + core) * TOK + start, (chip + 1 - core) * TOK + start]
        return input_product(pieces, starts, weight, before)

    input_grad = gathered(((0, 0, grad_out), (1, 0, ahead_early), (3, half, behind_late)), None)
    ahead_early, behind_late, input_grad = lax.optimization_barrier((ahead_early, behind_late, input_grad))
    far_early, far_late = fetch(ahead_early, "x", 1), fetch(behind_late, "x", -1)
    moment, far_early, far_late = lax.optimization_barrier((moment, far_early, far_late))
    moment_tops = exchange(jnp.broadcast_to(jnp.max(jnp.abs(moment)), (N_DEV, LANES)))
    others = ((1, half, ahead_late), (3, 0, behind_early), (2, 0, far_early), (2, half, far_late))
    input_grad = gathered(others, input_grad)
    moment_tops, input_grad = lax.optimization_barrier((moment_tops, input_grad))
    new_scale = quant_top / (jnp.max(moment_tops) + peak_eps)
    new_moment_q = (moment * new_scale).astype(jnp.bfloat16)
    return (input_grad, new_master, new_moment_q, new_second, new_scale, grad_scale, new_weight)


def solution(mesh):
    fine = Mesh(mesh.devices.reshape(SIDE, SIDE, SIDE, 2), EVERY)
    dp, mp = ("y", "z"), MP_AXES
    return jax.shard_map(
        local,
        mesh=fine,
        in_specs=(
            P(dp + mp, None),
            P(dp, mp),
            P(None, mp),
            P(dp, mp),
            P(dp, mp),
            P(dp, mp),
            P(),
            P(),
        ),
        out_specs=(
            P(dp, mp),
            P(dp, mp),
            P(dp, mp),
            P(dp, mp),
            P(),
            P(),
            P(None, mp),
        ),
        check_vma=False,
    )
```
